256 devices in a mesh: leaf: 8 (over z), blk: 32 (over x, y, core).
Axes of the slice: x: 4, y: 4, z: 8, core: 2. Of those that a mesh axis runs over, the one named last changes fastest.
Arguments:
- root_sigma: float32 [2, 256, 256], replicated, as said below
- top_inv: bfloat16 [8, 2, 256, 256], P('leaf'), as said below
- top_panels: bfloat16 [8, 2, 256, 256], P('leaf')
- top_parents: int32 [8, 2], P('leaf'), may hold values from 0 to 1
- sub_inv: bfloat16 [8, 32, 2, 256, 256], P('leaf', 'blk'), as said below
- sub_panels: bfloat16 [8, 32, 2, 256, 256], P('leaf', 'blk')
- sub_parents: int32 [8, 32, 2], P('leaf', 'blk'), may hold values from 0 to 1
Outputs:
- sub_sigma: float32 [8, 32, 2, 256, 256], P('leaf', 'blk')
- top_sigma: float32 [8, 2, 256, 256], P('leaf')
The draws below stay inside these ranges and needn't reach their ends.
Inputs may be any that keep to these rules, and one draw needn't show every extreme that they name: `root_sigma`: every block is symmetric. `top_inv`: every block is lower triangular with a positive diagonal. `sub_inv`: every block is lower triangular with a positive diagonal.
All inputs are finite; a program needn't handle non-finite values.
Results may differ from the reference program's by a relative error of at most 0.0003.
Values may be sent and summed in bfloat16 or wider, within the bound.
A program may use at most 64 MiB of HBM per device.

```python
import math
import jax
import jax.numpy as jnp
from jax import lax

B = 256
NB = 2
N_LEAF = 8
N_BLK = 32


def make_inverse(key, lead):
    shape = tuple(lead) + (B, B)
    first, second = jax.random.split(jax.random.fold_in(key, 21), 2)
    gains = jax.random.uniform(first, tuple(lead) + (B,), jnp.float32, 0.5, 1.0)
    rows_idx = jnp.arange(B, dtype=jnp.int32)[:, None]
    cols_idx = jnp.arange(B, dtype=jnp.int32)[None, :]
    lower = (rows_idx > cols_idx).astype(jnp.float32)
    noise_part = jax.random.normal(second, shape, jnp.float32) * (0.3 / math.sqrt(B)) * lower
    eye_matrix = jnp.eye(B, dtype=jnp.float32)
    return eye_matrix * gains[..., None] + noise_part


def make_root(key):
    shape = (NB, B, B)
    first, second = jax.random.split(jax.random.fold_in(key, 17), 2)
    gains = jax.random.uniform(first, (NB, B), jnp.float32, 0.5, 1.5)
    noise_part = jax.random.normal(second, shape, jnp.float32) * (0.1 / math.sqrt(B))
    noise_part = noise_part + jnp.swapaxes(noise_part, 1, 2)
    eye_matrix = jnp.eye(B, dtype=jnp.float32)
    return eye_matrix * gains[..., None] + noise_part


def make_panels(key, lead):
    shape = tuple(lead) + (B, B)
    first, second, third, fourth, fifth = jax.random.split(jax.random.fold_in(key, 33), 5)
    share_slow = 0.5
    slow_mask = jax.random.uniform(first, (B,), jnp.float32) < share_slow
    fast_rates = jax.random.uniform(second, (B,), jnp.float32, 0.3, 0.7)
    slow_rates = jnp.exp(-jax.random.uniform(third, (B,), jnp.float32, 0.0, 0.8) / 12.0)
    column_rates = jnp.where(slow_mask, slow_rates, fast_rates)
    offsets = jax.random.randint(fourth, tuple(lead) + (1, 1), 1, B)
    rows_idx = jnp.arange(B, dtype=jnp.int32)[:, None]
    cols_idx = jnp.arange(B, dtype=jnp.int32)[None, :]
    cyclic = ((cols_idx - rows_idx - offsets) % B == 0).astype(jnp.float32)
    base_matrix = 0.75 * jnp.eye(B, dtype=jnp.float32) + 0.2 * cyclic
    noise_part = jax.random.normal(fifth, shape, jnp.float32) * (0.01 / math.sqrt(B))
    return base_matrix * column_rates[None, :] + noise_part


def draw_root_sigma(key, part):
    return make_root(jax.random.fold_in(key, 1))


def draw_top_inv(key, part):
    return make_inverse(jax.random.fold_in(key, 2), (N_LEAF, NB)).astype(jnp.bfloat16)


def draw_top_panels(key, part):
    return make_panels(jax.random.fold_in(key, 3), (N_LEAF, NB)).astype(jnp.bfloat16)


def draw_sub_inv(key, part):
    return make_inverse(jax.random.fold_in(key, 4), (N_LEAF, N_BLK, NB)).astype(jnp.bfloat16)


def draw_sub_panels(key, part):
    return make_panels(jax.random.fold_in(key, 5), (N_LEAF, N_BLK, NB)).astype(jnp.bfloat16)


def plant(entries, key, smallest, high):
    dims = entries.shape
    spot = [jax.random.randint(jax.random.fold_in(key, axis), (), 0, dims[axis]) for axis in range(len(dims))]
    entries = entries.at[tuple(spot)].set(smallest)
    longest = dims.index(max(dims))
    spot[longest] = (spot[longest] + 1) % dims[longest]
    return entries.at[tuple(spot)].set(high)


def setup_inputs(seed: int = 0) -> dict:
    streams_of = jax.random.split(jax.random.key(seed), 8)
    root_sigma = draw_root_sigma(jax.random.fold_in(streams_of[7], 71), 0)
    top_inv = draw_top_inv(jax.random.fold_in(streams_of[7], 71), 0)
    top_panels = draw_top_panels(jax.random.fold_in(streams_of[7], 71), 0)
    top_parents = plant(jax.random.randint(streams_of[3], (N_LEAF, NB), 0, NB), jax.random.fold_in(streams_of[3], 1), 0, NB - 1).astype(jnp.int32)
    sub_inv = draw_sub_inv(jax.random.fold_in(streams_of[7], 71), 0)
    sub_panels = draw_sub_panels(jax.random.fold_in(streams_of[7], 71), 0)
    sub_parents = plant(jax.random.randint(streams_of[6], (N_LEAF, N_BLK, NB), 0, NB), jax.random.fold_in(streams_of[6], 1), 0, NB - 1).astype(jnp.int32)
    return dict(root_sigma=root_sigma, top_inv=top_inv, top_panels=top_panels, top_parents=top_parents, sub_inv=sub_inv, sub_panels=sub_panels, sub_parents=sub_parents)


HIGH = lax.Precision.HIGHEST


def parent_table(parents, node_count):
    return (parents[:, None] == jnp.arange(node_count, dtype=jnp.int32)[None, :]).astype(jnp.float32)


def apply_node(inverse, panels, parent_hot, above):
    picked = jnp.einsum('kn,nij->kij', parent_hot, above, precision=HIGH)
    wide_inv = inverse.astype(jnp.float32)
    wide_pan = panels.astype(jnp.float32)
    carried = jnp.einsum('kij,kjm->kim', wide_pan, wide_inv, precision=HIGH)
    own_part = jnp.einsum('kji,kjm->kim', wide_inv, wide_inv, precision=HIGH)
    inner_sum = jnp.einsum('kij,kjm->kim', picked, carried, precision=HIGH)
    return own_part + jnp.einsum('kji,kjm->kim', carried, inner_sum, precision=HIGH)


def tree_parent(index):
    return index - (1 << (index.bit_length() - 1))


def reference(root_sigma, top_inv, top_panels, top_parents, sub_inv, sub_panels, sub_parents):
    node_count = root_sigma.shape[0]
    top_list = []
    for group in range(N_LEAF):
        above = root_sigma.astype(jnp.float32) if group == 0 else top_list[tree_parent(group)]
        top_list.append(apply_node(top_inv[group], top_panels[group],
                                   parent_table(top_parents[group], node_count), above))
    sub_list = []
    for group in range(N_LEAF):
        group_list = []
        for member in range(N_BLK):
            above = top_list[group] if member == 0 else group_list[tree_parent(member)]
            group_list.append(apply_node(sub_inv[group, member], sub_panels[group, member],
                                         parent_table(sub_parents[group, member], node_count), above))
        sub_list.append(jnp.stack(group_list))
    return jnp.stack(sub_list), jnp.stack(top_list)
```

```python
import functools

import jax
import jax.numpy as jnp
from jax import lax
from jax.experimental import pallas as pl
from jax.experimental.pallas import tpu as pltpu
from jax.sharding import PartitionSpec as P

MESH = pl.DeviceIdType.MESH
F32 = jnp.float32
BF16 = jnp.bfloat16
B = 256
H = 128
ROWS = 896
CH = 8
CROWS = ROWS // CH
ZCH = CH // 2

T0, T1, T2, T3, TOWN, RX, R1, OWN, Y0, Y1, D0 = range(11)
NSLOT = 11
(S_T0P, S_T0M, S_T1, S_T2, S_T3, S_D0, S_D1, S_D2, S_D3,
 S_XA, S_XB, S_R1, S_YA, S_YB, S_Y1, S_DD) = range(16)
NSEND = 16


def split(value):
    high = value.astype(BF16)
    return high, (value - high.astype(F32)).astype(BF16)


def pick(options, index):
    result = jnp.int32(options[0])
    for at in range(1, len(options)):
        result = jnp.where(index == at, jnp.int32(options[at]), result)
    return result


def kernel(root_ref, tinv_ref, tpan_ref, tpar_ref, sinv_ref, span_ref, spar_ref,
           sub_ref, top_ref, slots, x_ref, send_sem, recv_sem):
    z = lax.axis_index("leaf")
    blk = lax.axis_index("blk")
    x = blk // 8
    y = (blk // 2) % 4
    c = blk % 2

    def dev(zz, xx, yy, cc):
        return (zz, xx * 8 + yy * 2 + cc)

    zp, zm = dev((z + 1) % 8, x, y, c), dev((z + 7) % 8, x, y, c)
    xp, xm = dev(z, (x + 1) % 4, y, c), dev(z, (x + 3) % 4, y, c)
    yp, ym = dev(z, x, (y + 1) % 4, c), dev(z, x, (y + 3) % 4, c)
    other = dev(z, x, y, 1 - c)

    barrier = pltpu.get_barrier_semaphore()
    for where in (zp, zm, xp, xm, yp, ym, other):
        pl.semaphore_signal(barrier, inc=1, device_id=where, device_id_type=MESH)

    rows_at = lax.broadcasted_iota(jnp.int32, (H, H), 0)
    cols_at = lax.broadcasted_iota(jnp.int32, (H, H), 1)
    corner = (rows_at == 0) & (cols_at == H - 1)

    def pack(inv, pan, par, slot):
        slots[slot, 0:B, :] = pan(0)
        slots[slot, B:2 * B, :] = pan(1)
        for k in range(2):
            v = inv(k)
            slots[slot, 2 * B + k * H:2 * B + (k + 1) * H, :] = v[H:, :]
            quarter = jnp.where(corner, par(k).astype(F32), v[:H, :H].astype(F32))
            slots[slot, 3 * B:3 * B + H, k * H:(k + 1) * H] = quarter.astype(BF16)

    pack(lambda k: tinv_ref[0, k], lambda k: tpan_ref[0, k], lambda k: tpar_ref[0, k],
         jnp.minimum(z, 4))
    pack(lambda k: sinv_ref[0, 0, k], lambda k: span_ref[0, 0, k], lambda k: spar_ref[0, 0, k],
         RX + jnp.minimum(x, 2))
    x_ref[...] = root_ref[...]

    pl.semaphore_wait(barrier, 7)

    def copy(src, dst, k, sid, where):
        rows = pl.ds(pl.multiple_of(k * CROWS, CROWS), CROWS)
        return pltpu.make_async_remote_copy(
            src_ref=slots.at[src, rows, :], dst_ref=slots.at[dst, rows, :],
            send_sem=send_sem.at[sid, k], recv_sem=recv_sem.at[dst, k],
            device_id=where, device_id_type=MESH)

    def arrived(slot, k):
        copy(slot, slot, k, 0, other).wait_recv()

    zflows = (
        (T0, jnp.where(z < 4, z, 8 - z), z >= 0, z >= 1,
         ((S_T0P, zp, z < 3), (S_T0M, zm, (z == 0) | (z > 4)))),
        (T1, z - 1, z >= 1, (z == 3) | (z == 5) | (z == 7), ((S_T1, zp, z < 7),)),
        (T2, (10 - z) % 8, (10 - z) % 8 <= 4, z == 6, ((S_T2, zm, z != 6),)),
        (T3, z - 3, z >= 3, z == 7, ((S_T3, zp, z < 7),)),
    )
    rx_depth = pick((0, 1, 2, 1), x)
    y0_depth = rx_depth + pick((0, 1, 2, 1), y)
    y1_depth = rx_depth + y - 1

    pflows = (
        (RX, rx_depth, x >= 0, (
            (RX, S_XA, xp, x == 0), (RX, S_XB, xm, (x == 0) | (x == 3)),
            (Y0, S_YA, yp, y == 0), (Y0, S_YB, ym, y == 0),
            (Y1, S_Y1, yp, y == 1), (D0, S_DD, other, (c == 0) & (y == 0)))),
        (R1, x - 1, x >= 1, ((R1, S_R1, xp, x < 3),)),
        (Y0, y0_depth, y >= 1, (
            (Y0, S_YB, ym, y == 3), (D0, S_DD, other, c == 0))),
        (Y1, y1_depth, y >= 2, ((Y1, S_Y1, yp, y == 2),)),
        (D0, jnp.where(y == 0, rx_depth, y0_depth) + 1, c == 1, ()),
    )

    def relay(t, carry):
        for at, (slot, depth, member, needed, outs) in enumerate(zflows):
            j = t - depth

            @pl.when(member & (j >= 0) & (j < ZCH))
            def _():
                k = c * ZCH + j

                @pl.when(depth > 0)
                def _():
                    arrived(slot, k)

                for sid, where, when in outs:
                    @pl.when(when)
                    def _():
                        copy(slot, slot, k, sid, where).start()

                @pl.when(needed & (depth > 0))
                def _():
                    copy(slot, slot, k, S_D0 + at, other).start()

        for slot, depth, member, outs in pflows:
            k = t - depth

            @pl.when(member & (k >= 0) & (k < CH))
            def _():
                @pl.when(depth > 0)
                def _():
                    arrived(slot, k)

                for dst, sid, where, when in outs:
                    @pl.when(when)
                    def _():
                        copy(slot, dst, k, sid, where).start()
        return carry

    lax.fori_loop(0, CH + 5, relay, 0)

    def late(j, carry):
        for slot, depth, member, needed, outs in zflows:
            @pl.when(needed & (depth > 0))
            def _():
                arrived(slot, (1 - c) * ZCH + j)
        return carry

    lax.fori_loop(0, ZCH, late, 0)

    tri = rows_at >= cols_at

    def step(s, carry):
        slot = pick((T0, T1, jnp.int32(2) + z % 2, TOWN, D0, jnp.where(y == 0, RX, Y0), Y1, RX, R1,
                     jnp.where(x == 1, R1, OWN)), s)
        active = pick((1, z % 2, (z // 2) % 2, z // 4, c, 1, (y == 3).astype(jnp.int32),
                       (y >= 1).astype(jnp.int32), (x == 3).astype(jnp.int32),
                       (x >= 1).astype(jnp.int32)), s)

        @pl.when(active == 1)
        def _():
            above0, above1 = x_ref[0], x_ref[1]
            for k in range(2):
                panel = slots[slot, k * B:(k + 1) * B, :]
                low = slots[slot, 2 * B + k * H:2 * B + (k + 1) * H, :]
                quarter = slots[slot, 3 * B:3 * B + H, k * H:(k + 1) * H].astype(F32)
                second = quarter[0:1, H - 1:H] > 0.5
                quarter = jnp.where(tri, quarter, 0.0).astype(BF16)
                v = jnp.concatenate(
                    [jnp.concatenate([quarter, jnp.zeros((H, H), BF16)], axis=1), low], axis=0)
                own = lax.dot_general(v, v, (((0,), (0,)), ((), ())), preferred_element_type=F32)
                carried = jnp.dot(panel, v, preferred_element_type=F32)
                ch, cl = split(carried)
                th, tl = split(carried.T)
                xh, xl = split(jnp.where(second, above1, above0))
                u = jnp.dot(jnp.concatenate([th, tl, th], axis=1),
                            jnp.concatenate([xh, xh, xl], axis=0), preferred_element_type=F32)
                uh, ul = split(u)
                x_ref[k] = own + jnp.dot(
                    jnp.concatenate([uh, ul, uh], axis=1),
                    jnp.concatenate([ch, ch, cl], axis=0), preferred_element_type=F32)

        @pl.when(s == 3)
        def _():
            top_ref[0] = x_ref[...]
        return carry

    lax.fori_loop(0, 10, step, 0)
    sub_ref[0, 0] = x_ref[...]

    def drain_z(j, carry):
        for at, (slot, depth, member, needed, outs) in enumerate(zflows):
            @pl.when(member)
            def _():
                k = c * ZCH + j
                for sid, where, when in outs:
                    @pl.when(when)
                    def _():
                        copy(slot, slot, k, sid, where).wait_send()

                @pl.when(needed & (depth > 0))
                def _():
                    copy(slot, slot, k, S_D0 + at, other).wait_send()
        return carry

    def drain_p(k, carry):
        for slot, depth, member, outs in pflows:
            @pl.when(member)
            def _():
                for dst, sid, where, when in outs:
                    @pl.when(when)
                    def _():
                        copy(slot, dst, k, sid, where).wait_send()
        return carry

    lax.fori_loop(0, ZCH, drain_z, 0)
    lax.fori_loop(0, CH, drain_p, 0)


def on_device(root_sigma, top_inv, top_panels, top_parents, sub_inv, sub_panels, sub_parents):
    vmem = pl.BlockSpec(memory_space=pltpu.VMEM)
    smem = pl.BlockSpec(memory_space=pltpu.SMEM)
    return pl.pallas_call(
        kernel,
        out_shape=(jax.ShapeDtypeStruct((1, 1, 2, B, B), F32),
                   jax.ShapeDtypeStruct((1, 2, B, B), F32)),
        in_specs=[vmem, vmem, vmem, smem, vmem, vmem, smem],
        out_specs=(vmem, vmem),
        scratch_shapes=[
            pltpu.VMEM((NSLOT, ROWS, B), BF16),
            pltpu.VMEM((2, B, B), F32),
            pltpu.SemaphoreType.DMA((NSEND, CH)),
            pltpu.SemaphoreType.DMA((NSLOT, CH)),
        ],
        compiler_params=pltpu.CompilerParams(
            collective_id=0, has_side_effects=True, vmem_limit_bytes=40 << 20),
    )(root_sigma, top_inv, top_panels, top_parents, sub_inv, sub_panels, sub_parents)


def solution(mesh):
    in_specs = (
        P(),
        P("leaf", None, None, None),
        P("leaf", None, None, None),
        P("leaf", None),
        P("leaf", "blk", None, None, None),
        P("leaf", "blk", None, None, None),
        P("leaf", "blk", None),
    )
    out_specs = (P("leaf", "blk", None, None, None), P("leaf", None, None, None))
    return jax.shard_map(
        on_device, mesh=mesh, in_specs=in_specs, out_specs=out_specs, check_vma=False
    )
```

```python
import functools

import jax
import jax.numpy as jnp
from jax import lax
from jax.experimental import pallas as pl
from jax.experimental.pallas import tpu as pltpu
from jax.sharding import PartitionSpec as P

MESH = pl.DeviceIdType.MESH
F32 = jnp.float32
BF16 = jnp.bfloat16
B = 256
H = 128
ROWS = 896
CH = 7
ZCH = 2
PACE = 2
ZHOP, ZSTEP = 2, 1
ZUP = ZCH // 2
LAST = max(CH + 5, 4 * ZHOP + ZSTEP * ZCH)

T0, T1, T2, T3, TOWN, RX, R1, OWN, Y0, Y1, D0 = range(11)
NSLOT = 11
(S_T0P, S_T0M, S_T1, S_T2, S_T3, S_D0, S_D1, S_D2, S_D3,
 S_XA, S_XB, S_R1, S_YA, S_YB, S_Y1, S_DD, S_T1M, S_T2M) = range(18)
NSEND = 18


def split(value):
    high = value.astype(BF16)
    return high, (value - high.astype(F32)).astype(BF16)


def pick(options, index):
    result = jnp.int32(options[0])
    for at in range(1, len(options)):
        result = jnp.where(index == at, jnp.int32(options[at]), result)
    return result


def kernel(root_ref, tinv_ref, tpan_ref, tpar_ref, sinv_ref, span_ref, spar_ref,
           sub_ref, top_ref, slots, x_ref, own_ref, left_ref, right_ref,
           corners, tpar, spar, local_sem, send_sem, recv_sem):
    z = lax.axis_index("leaf")
    blk = lax.axis_index("blk")
    x = blk // 8
    y = (blk // 2) % 4
    c = blk % 2

    def dev(zz, xx, yy, cc):
        return (zz, xx * 8 + yy * 2 + cc)

    zp, zm = dev((z + 1) % 8, x, y, c), dev((z + 7) % 8, x, y, c)
    xp, xm = dev(z, (x + 1) % 4, y, c), dev(z, (x + 3) % 4, y, c)
    yp, ym = dev(z, x, (y + 1) % 4, c), dev(z, x, (y + 3) % 4, c)
    other = dev(z, x, y, 1 - c)

    barrier = pltpu.get_barrier_semaphore()
    for where in (zp, zm, xp, xm, yp, ym, other):
        pl.semaphore_signal(barrier, inc=1, device_id=where, device_id_type=MESH)

    top_slot = jnp.minimum(z, 4)
    sub_slot = RX + jnp.minimum(x, 2)
    loads = []

    def load(src, dst):
        loads.append(pltpu.make_async_copy(src, dst, local_sem.at[len(loads)]))
        loads[-1].start()

    load(tpar_ref, tpar)
    load(spar_ref, spar)
    for at, slot, inv, pan in ((0, top_slot, tinv_ref.at[0], tpan_ref.at[0]),
                               (1, sub_slot, sinv_ref.at[0, 0], span_ref.at[0, 0])):
        for k in range(2):
            load(inv.at[k, 0:H, 0:H], corners.at[at, k])
            load(pan.at[k], slots.at[slot, k * B:(k + 1) * B, :])
            load(inv.at[k, H:B, :], slots.at[slot, 2 * B + k * H:2 * B + (k + 1) * H, :])
    load(root_ref, x_ref)

    rows_at = lax.broadcasted_iota(jnp.int32, (H, H), 0)
    cols_at = lax.broadcasted_iota(jnp.int32, (H, H), 1)
    corner = (rows_at == 0) & (cols_at == H - 1)
    for copy_in in loads:
        copy_in.wait()
    for at, slot, par in ((0, top_slot, lambda k: tpar[0, k]), (1, sub_slot, lambda k: spar[0, 0, k])):
        for k in range(2):
            quarter = jnp.where(corner, par(k).astype(F32), corners[at, k].astype(F32))
            slots[slot, 3 * B:3 * B + H, k * H:(k + 1) * H] = quarter.astype(BF16)

    pl.semaphore_wait(barrier, 7)

    def copy(src, dst, k, sid, where, chunks=CH):
        size = ROWS // chunks
        rows = pl.ds(pl.multiple_of(k * size, size), size)
        return pltpu.make_async_remote_copy(
            src_ref=slots.at[src, rows, :], dst_ref=slots.at[dst, rows, :],
            send_sem=send_sem.at[sid], recv_sem=recv_sem.at[dst, k],
            device_id=where, device_id_type=MESH)

    def arrived(slot, k, chunks=CH):
        copy(slot, slot, k, 0, other, chunks).wait_recv()

    up2 = (z >= 2) & (z <= 6)
    zflows = (
        (T0, jnp.where(z < 4, z, 8 - z), z >= 0, 0, ZCH, z >= 1,
         ((S_T0P, zp, z < 3, 0, ZCH), (S_T0M, zm, (z == 0) | (z > 4), 0, ZCH))),
        (T1, pick((1, 0, 1, 2, 3, 4, 0, 2), z), z != 6, 0, ZCH, (z == 3) | (z == 5) | (z == 7),
         ((S_T1, zp, (z >= 1) & (z <= 4), 0, ZCH), (S_T1M, zm, z <= 1, 0, ZCH))),
        (T2, jnp.where(up2, z - 2, (10 - z) % 8), z >= 0,
         jnp.where(up2, 0, ZUP), jnp.where((z >= 3) & (z <= 5), ZUP, ZCH), z == 6,
         ((S_T2, zp, (z >= 2) & (z <= 5), 0, ZUP), (S_T2M, zm, (z <= 2) | (z == 7), ZUP, ZCH))),
        (T3, z - 3, z >= 3, 0, ZCH, z == 7, ((S_T3, zp, z < 7, 0, ZCH),)),
    )
    rx_depth = pick((0, 1, 2, 1), x)
    y0_depth = rx_depth + pick((0, 1, 2, 1), y)
    y1_depth = rx_depth + y - 1
    d0_depth = jnp.where(y == 0, rx_depth, y0_depth) + 1

    pflows = (
        (RX, rx_depth, x >= 0, (
            (RX, S_XA, xp, x == 0), (RX, S_XB, xm, (x == 0) | (x == 3)),
            (Y0, S_YA, yp, y == 0), (Y0, S_YB, ym, y == 0),
            (Y1, S_Y1, yp, y == 1), (D0, S_DD, other, (c == 0) & (y == 0)))),
        (R1, x - 1, x >= 1, ((R1, S_R1, xp, x < 3),)),
        (Y0, y0_depth, y >= 1, (
            (Y0, S_YB, ym, y == 3), (D0, S_DD, other, c == 0))),
        (Y1, y1_depth, y >= 2, ((Y1, S_Y1, yp, y == 2),)),
    )

    def either(flags):
        return functools.reduce(jnp.logical_or, flags)

    def source(k, carry):
        for slot, depth, member, first, end, needed, outs in zflows:
            for sid, where, when, lo, hi in outs:
                @pl.when(member & (depth == 0) & when & (k >= lo) & (k < hi))
                def _():
                    copy(slot, slot, c * ZCH + k, sid, where, 2 * ZCH).start()
        for slot, depth, member, outs in pflows[:2]:
            for dst, sid, where, when in outs:
                @pl.when(member & (depth == 0) & when & (k < CH))
                def _():
                    copy(slot, dst, k, sid, where).start()
        return carry

    lax.fori_loop(0, max(CH, ZCH), source, 0)

    tri = rows_at >= cols_at

    after = lambda depth: ZHOP * depth + ZSTEP * ZCH
    plan = (
        (TOWN, z >= 4, 0, 0),
        (OWN, x >= 2, 0, 0),
        (T0, z >= 0, jnp.where(z > 0, after(zflows[0][1]), 0), jnp.where(z > 0, ZCH, 0)),
        (T1, z % 2 == 1, jnp.where(z > 1, after(zflows[1][1]), 0), jnp.where(z > 1, ZCH, 0)),
        (T2, z % 4 == 2, jnp.where(z > 2, after(zflows[2][1]), 0), jnp.where(z > 2, ZCH, 0)),
        (T3, z % 4 == 3, jnp.where(z > 3, after(zflows[3][1]), 0), jnp.where(z > 3, ZCH, 0)),
        (RX, x >= 0, jnp.where(x > 0, rx_depth + CH, 0),
         jnp.where((y >= 2) & ((x == 1) | (x == 2)), CH, 0)),
        (R1, x % 2 == 1, jnp.where(x > 1, x - 1 + CH, 0), jnp.where(x == 3, CH, 0)),
        (Y0, y >= 1, y0_depth + CH, jnp.where((y < 3) & (c == 1), CH, 0)),
        (Y1, y == 3, y1_depth + CH, CH),
        (D0, c == 1, d0_depth + CH, CH),
    )
    prep_ready, latest = [], jnp.int32(0)
    at_slot = {}
    for slot, needed, when, count in plan:
        latest = jnp.where(needed, jnp.maximum(latest, when), latest)
        prep_ready.append(latest)
        at_slot[slot] = latest

    def prepare(at, carry):
        slot = pick([entry[0] for entry in plan], at)

        @pl.when(pick([entry[1].astype(jnp.int32) for entry in plan], at) == 1)
        def _():
            def await_half(k, carry):
                arrived(slot, (1 - c) * ZCH + k, 2 * ZCH)
                return carry

            def await_chunk(k, carry):
                arrived(slot, k)
                return carry

            count = pick([entry[3] for entry in plan], at)
            lax.fori_loop(0, jnp.where(slot <= TOWN, count, 0), await_half, 0)
            lax.fori_loop(0, jnp.where(slot <= TOWN, 0, count), await_chunk, 0)
            for k in range(2):
                panel = slots[slot, k * B:(k + 1) * B, :]
                low = slots[slot, 2 * B + k * H:2 * B + (k + 1) * H, :]
                quarter = slots[slot, 3 * B:3 * B + H, k * H:(k + 1) * H].astype(F32)
                quarter = jnp.where(tri, quarter, 0.0).astype(BF16)
                v = jnp.concatenate(
                    [jnp.concatenate([quarter, jnp.zeros((H, H), BF16)], axis=1), low], axis=0)
                own_ref[slot, k] = lax.dot_general(
                    v, v, (((0,), (0,)), ((), ())), preferred_element_type=F32)
                carried = jnp.dot(panel, v, preferred_element_type=F32)
                ch, cl = split(carried)
                th, tl = split(carried.T)
                left_ref[slot, k] = jnp.concatenate([th, tl, th], axis=1)
                right_ref[slot, k] = jnp.concatenate([ch, ch, cl], axis=0)
        return carry

    chain_slot = (T0, T1, 2 + z % 2, TOWN, D0, jnp.where(y == 0, RX, Y0), Y1, RX, R1,
                  jnp.where(x == 1, R1, OWN))
    chain_on = (z >= 0, z % 2 == 1, (z // 2) % 2 == 1, z >= 4, c == 1, y >= 0, y == 3, y >= 1,
                x == 3, x >= 1)
    chain_at = (at_slot[T0], at_slot[T1], jnp.where(z % 2 == 0, at_slot[T2], at_slot[T3]), at_slot[TOWN],
                at_slot[D0], jnp.where(y == 0, at_slot[RX], at_slot[Y0]), at_slot[Y1], at_slot[RX],
                at_slot[R1], jnp.where(x == 1, at_slot[R1], at_slot[OWN]))
    ready, latest = [], jnp.int32(0)
    for s in range(10):
        latest = jnp.where(chain_on[s], jnp.maximum(latest, chain_at[s]), latest)
        ready.append(latest)

    def step(s, carry):
        slot = pick(chain_slot, s)

        @pl.when(pick([flag.astype(jnp.int32) for flag in chain_on], s) == 1)
        def _():
            above0, above1 = x_ref[0], x_ref[1]
            for k in range(2):
                quarter = slots[slot, 3 * B:3 * B + 16, k * H:(k + 1) * H].astype(F32)
                second = quarter[0:1, H - 1:H] > 0.5
                xh, xl = split(jnp.where(second, above1, above0))
                u = jnp.dot(left_ref[slot, k], jnp.concatenate([xh, xh, xl], axis=0),
                            preferred_element_type=F32)
                uh, ul = split(u)
                x_ref[k] = own_ref[slot, k] + jnp.dot(
                    jnp.concatenate([uh, ul, uh], axis=1), right_ref[slot, k],
                    preferred_element_type=F32)

        @pl.when(s == 3)
        def _():
            top_ref[0] = x_ref[...]
        return carry

    def relay(t, carry):
        prepared, done = carry

        for at, (slot, depth, member, first, end, needed, outs) in enumerate(zflows):
            late_by = t - ZHOP * depth
            j = late_by // ZSTEP

            @pl.when(member & (depth > 0) & (late_by % ZSTEP == 0) & (j >= first) & (j < end))
            def _():
                k = c * ZCH + j
                arrived(slot, k, 2 * ZCH)
                for sid, where, when, lo, hi in outs:
                    @pl.when(when)
                    def _():
                        copy(slot, slot, k, sid, where, 2 * ZCH).start()

                @pl.when(needed)
                def _():
                    copy(slot, slot, k, S_D0 + at, other, 2 * ZCH).start()

        for slot, depth, member, outs in pflows:
            k = t - depth

            @pl.when(member & (depth > 0) & (k >= 0) & (k < CH) & either([o[3] for o in outs]))
            def _():
                arrived(slot, k)
                for dst, sid, where, when in outs:
                    @pl.when(when)
                    def _():
                        copy(slot, dst, k, sid, where).start()

        def so_far(times):
            count = jnp.int32(0)
            for time in times:
                count += (time <= t).astype(jnp.int32)
            return count

        now = so_far(prep_ready)
        lax.fori_loop(prepared, now, prepare, 0)
        count = so_far(ready)
        count = jnp.where(t >= LAST, 10, jnp.minimum(count, done + PACE))
        lax.fori_loop(done, count, step, 0)
        return now, count

    lax.fori_loop(0, LAST + 1, relay, (jnp.int32(0), jnp.int32(0)))
    sub_ref[0, 0] = x_ref[...]

    def gone(sid, rows):
        part = slots.at[0, pl.ds(0, rows), :]
        pltpu.make_async_remote_copy(
            src_ref=part, dst_ref=part, send_sem=send_sem.at[sid], recv_sem=recv_sem.at[0, 0],
            device_id=other, device_id_type=MESH).wait_send()

    for at, (slot, depth, member, first, end, needed, outs) in enumerate(zflows):
        for sid, where, when, lo, hi in outs:
            @pl.when(member & when)
            def _():
                gone(sid, (hi - lo) * (ROWS // 2 // ZCH))

        @pl.when(needed & (depth > 0))
        def _():
            gone(S_D0 + at, ROWS // 2)

    streams = {}
    for slot, depth, member, outs in pflows:
        for dst, sid, where, when in outs:
            streams.setdefault(sid, []).append(member & when)
    for sid, flags in streams.items():
        @pl.when(either(flags))
        def _():
            gone(sid, ROWS)


def on_device(root_sigma, top_inv, top_panels, top_parents, sub_inv, sub_panels, sub_parents):
    vmem = pl.BlockSpec(memory_space=pltpu.VMEM)
    hbm = pl.BlockSpec(memory_space=pltpu.HBM)
    arrays = [pltpu.with_memory_space_constraint(a, pltpu.HBM) for a in
              (root_sigma, top_inv, top_panels, top_parents, sub_inv, sub_panels, sub_parents)]
    return pl.pallas_call(
        kernel,
        out_shape=(jax.ShapeDtypeStruct((1, 1, 2, B, B), F32),
                   jax.ShapeDtypeStruct((1, 2, B, B), F32)),
        in_specs=[hbm] * 7,
        out_specs=(vmem, vmem),
        scratch_shapes=[
            pltpu.VMEM((NSLOT, ROWS, B), BF16),
            pltpu.VMEM((2, B, B), F32),
            pltpu.VMEM((NSLOT, 2, B, B), F32),
            pltpu.VMEM((NSLOT, 2, B, 3 * B), BF16),
            pltpu.VMEM((NSLOT, 2, 3 * B, B), BF16),
            pltpu.VMEM((2, 2, H, H), BF16),
            pltpu.SMEM((1, 2), jnp.int32),
            pltpu.SMEM((1, 1, 2), jnp.int32),
            pltpu.SemaphoreType.DMA((15,)),
            pltpu.SemaphoreType.DMA((NSEND,)),
            pltpu.SemaphoreType.DMA((NSLOT, max(CH, 2 * ZCH))),
        ],
        compiler_params=pltpu.CompilerParams(
            collective_id=0, has_side_effects=True, vmem_limit_bytes=40 << 20),
    )(*arrays)


def solution(mesh):
    in_specs = (
        P(),
        P("leaf", None, None, None),
        P("leaf", None, None, None),
        P("leaf", None),
        P("leaf", "blk", None, None, None),
        P("leaf", "blk", None, None, None),
        P("leaf", "blk", None),
    )
    out_specs = (P("leaf", "blk", None, None, None), P("leaf", None, None, None))
    return jax.shard_map(
        on_device, mesh=mesh, in_specs=in_specs, out_specs=out_specs, check_vma=False
    )
```

```python
import functools

import jax
import jax.numpy as jnp
from jax import lax
from jax.experimental import pallas as pl
from jax.experimental.pallas import tpu as pltpu
from jax.sharding import PartitionSpec as P

MESH = pl.DeviceIdType.MESH
F32 = jnp.float32
BF16 = jnp.bfloat16
B = 256
H = 128
ROWS = 784
ZROWS = 832
CH = 7
ZCH = 2
PACE = 2
ZHOP, ZSTEP = 2, 1
ZUP = ZCH // 2
LAST = max(CH + 5, 4 * ZHOP + ZSTEP * ZCH)

T0, T1, T2, T3, TOWN, RX, R1, OWN, Y0, Y1, D0 = range(11)
NSLOT = 11
(S_T0P, S_T0M, S_T1, S_T2, S_T3, S_D0, S_D1, S_D2, S_D3,
 S_XA, S_XB, S_R1, S_YA, S_YB, S_Y1, S_DD, S_T1M, S_T2M) = range(18)
NSEND = 18


def split(value):
    high = value.astype(BF16)
    return high, (value - high.astype(F32)).astype(BF16)


def pick(options, index):
    result = jnp.int32(options[0])
    for at in range(1, len(options)):
        result = jnp.where(index == at, jnp.int32(options[at]), result)
    return result


def kernel(root_ref, tinv_ref, tpan_ref, tpar_ref, sinv_ref, span_ref, spar_ref,
           sub_ref, top_ref, slots, x_ref, own_ref, left_ref, right_ref,
           corners, tpar, spar, local_sem, send_sem, recv_sem):
    z = lax.axis_index("leaf")
    blk = lax.axis_index("blk")
    x = blk // 8
    y = (blk // 2) % 4
    c = blk % 2

    def dev(zz, xx, yy, cc):
        return (zz, xx * 8 + yy * 2 + cc)

    zp, zm = dev((z + 1) % 8, x, y, c), dev((z + 7) % 8, x, y, c)
    xp, xm = dev(z, (x + 1) % 4, y, c), dev(z, (x + 3) % 4, y, c)
    yp, ym = dev(z, x, (y + 1) % 4, c), dev(z, x, (y + 3) % 4, c)
    other = dev(z, x, y, 1 - c)

    barrier = pltpu.get_barrier_semaphore()
    for where in (zp, zm, xp, xm, yp, ym, other):
        pl.semaphore_signal(barrier, inc=1, device_id=where, device_id_type=MESH)

    top_slot = jnp.minimum(z, 4)
    sub_slot = RX + jnp.minimum(x, 2)
    loads = []

    def load(src, dst):
        loads.append(pltpu.make_async_copy(src, dst, local_sem.at[len(loads)]))
        loads[-1].start()

    load(tpar_ref, tpar)
    load(spar_ref, spar)
    for at, slot, inv, pan in ((0, top_slot, tinv_ref.at[0], tpan_ref.at[0]),
                               (1, sub_slot, sinv_ref.at[0, 0], span_ref.at[0, 0])):
        for k in range(2):
            load(inv.at[k, 0:H, 0:H], corners.at[at, k, 0])
            load(inv.at[k, H:B, H:B], corners.at[at, k, 1])
            load(pan.at[k], slots.at[slot, k * B:(k + 1) * B, :])
            load(inv.at[k, H:B, 0:H], slots.at[slot, 2 * B:2 * B + H, k * H:(k + 1) * H])
    load(root_ref, x_ref)

    rows_at = lax.broadcasted_iota(jnp.int32, (H, H), 0)
    cols_at = lax.broadcasted_iota(jnp.int32, (H, H), 1)
    tri = rows_at >= cols_at
    above = rows_at < cols_at
    even = rows_at == cols_at
    tile_row = lax.broadcasted_iota(jnp.int32, (16, H), 0)
    for copy_in in loads:
        copy_in.wait()
    for at, slot, par in ((0, top_slot, lambda k: tpar[0, k]), (1, sub_slot, lambda k: spar[0, 0, k])):
        for k in range(2):
            first, second = corners[at, k, 0].astype(F32), corners[at, k, 1].astype(F32)
            folded = jnp.where(above, second.T, first)
            slots[slot, 2 * B + H:3 * B, k * H:(k + 1) * H] = folded.astype(BF16)
            diagonal = jnp.sum(jnp.where(even, second, 0.0), axis=0, keepdims=True)
            tile = jnp.where(tile_row == 0, diagonal, par(k).astype(F32))
            slots[slot, 3 * B:ROWS, k * H:(k + 1) * H] = tile.astype(BF16)
    slots[top_slot, ROWS:ZROWS, :] = jnp.zeros((ZROWS - ROWS, B), BF16)

    pl.semaphore_wait(barrier, 7)

    def copy(src, dst, k, sid, where, chunks=CH):
        size = (ROWS if chunks == CH else ZROWS) // chunks
        rows = pl.ds(pl.multiple_of(k * size, size), size)
        return pltpu.make_async_remote_copy(
            src_ref=slots.at[src, rows, :], dst_ref=slots.at[dst, rows, :],
            send_sem=send_sem.at[sid], recv_sem=recv_sem.at[dst, k],
            device_id=where, device_id_type=MESH)

    def arrived(slot, k, chunks=CH):
        copy(slot, slot, k, 0, other, chunks).wait_recv()

    up2 = (z >= 2) & (z <= 6)
    zflows = (
        (T0, jnp.where(z < 4, z, 8 - z), z >= 0, 0, ZCH, z >= 1,
         ((S_T0P, zp, z < 3, 0, ZCH), (S_T0M, zm, (z == 0) | (z > 4), 0, ZCH))),
        (T1, pick((1, 0, 1, 2, 3, 4, 0, 2), z), z != 6, 0, ZCH, (z == 3) | (z == 5) | (z == 7),
         ((S_T1, zp, (z >= 1) & (z <= 4), 0, ZCH), (S_T1M, zm, z <= 1, 0, ZCH))),
        (T2, jnp.where(up2, z - 2, (10 - z) % 8), z >= 0,
         jnp.where(up2, 0, ZUP), jnp.where((z >= 3) & (z <= 5), ZUP, ZCH), z == 6,
         ((S_T2, zp, (z >= 2) & (z <= 5), 0, ZUP), (S_T2M, zm, (z <= 2) | (z == 7), ZUP, ZCH))),
        (T3, z - 3, z >= 3, 0, ZCH, z == 7, ((S_T3, zp, z < 7, 0, ZCH),)),
    )
    rx_depth = pick((0, 1, 2, 1), x)
    y0_depth = rx_depth + pick((0, 1, 2, 1), y)
    y1_depth = rx_depth + y - 1
    d0_depth = jnp.where(y == 0, rx_depth, y0_depth) + 1

    pflows = (
        (RX, rx_depth, x >= 0, (
            (RX, S_XA, xp, x == 0), (RX, S_XB, xm, (x == 0) | (x == 3)),
            (Y0, S_YA, yp, y == 0), (Y0, S_YB, ym, y == 0),
            (Y1, S_Y1, yp, y == 1), (D0, S_DD, other, (c == 0) & (y == 0)))),
        (R1, x - 1, x >= 1, ((R1, S_R1, xp, x < 3),)),
        (Y0, y0_depth, y >= 1, (
            (Y0, S_YB, ym, y == 3), (D0, S_DD, other, c == 0))),
        (Y1, y1_depth, y >= 2, ((Y1, S_Y1, yp, y == 2),)),
    )

    def either(flags):
        return functools.reduce(jnp.logical_or, flags)

    def source(k, carry):
        for slot, depth, member, first, end, needed, outs in zflows:
            for sid, where, when, lo, hi in outs:
                @pl.when(member & (depth == 0) & when & (k >= lo) & (k < hi))
                def _():
                    copy(slot, slot, c * ZCH + k, sid, where, 2 * ZCH).start()
        for slot, depth, member, outs in pflows[:2]:
            for dst, sid, where, when in outs:
                @pl.when(member & (depth == 0) & when & (k < CH))
                def _():
                    copy(slot, dst, k, sid, where).start()
        return carry

    lax.fori_loop(0, max(CH, ZCH), source, 0)

    after = lambda depth: ZHOP * depth + ZSTEP * ZCH
    plan = (
        (TOWN, z >= 4, 0, 0),
        (OWN, x >= 2, 0, 0),
        (T0, z >= 0, jnp.where(z > 0, after(zflows[0][1]), 0), jnp.where(z > 0, ZCH, 0)),
        (T1, z % 2 == 1, jnp.where(z > 1, after(zflows[1][1]), 0), jnp.where(z > 1, ZCH, 0)),
        (T2, z % 4 == 2, jnp.where(z > 2, after(zflows[2][1]), 0), jnp.where(z > 2, ZCH, 0)),
        (T3, z % 4 == 3, jnp.where(z > 3, after(zflows[3][1]), 0), jnp.where(z > 3, ZCH, 0)),
        (RX, x >= 0, jnp.where(x > 0, rx_depth + CH, 0),
         jnp.where((y >= 2) & ((x == 1) | (x == 2)), CH, 0)),
        (R1, x % 2 == 1, jnp.where(x > 1, x - 1 + CH, 0), jnp.where(x == 3, CH, 0)),
        (Y0, y >= 1, y0_depth + CH, jnp.where((y < 3) & (c == 1), CH, 0)),
        (Y1, y == 3, y1_depth + CH, CH),
        (D0, c == 1, d0_depth + CH, CH),
    )
    prep_ready, latest = [], jnp.int32(0)
    at_slot = {}
    for slot, needed, when, count in plan:
        latest = jnp.where(needed, jnp.maximum(latest, when), latest)
        prep_ready.append(latest)
        at_slot[slot] = latest

    def prepare(at, carry):
        slot = pick([entry[0] for entry in plan], at)

        @pl.when(pick([entry[1].astype(jnp.int32) for entry in plan], at) == 1)
        def _():
            def await_half(k, carry):
                arrived(slot, (1 - c) * ZCH + k, 2 * ZCH)
                return carry

            def await_chunk(k, carry):
                arrived(slot, k)
                return carry

            count = pick([entry[3] for entry in plan], at)
            lax.fori_loop(0, jnp.where(slot <= TOWN, count, 0), await_half, 0)
            lax.fori_loop(0, jnp.where(slot <= TOWN, 0, count), await_chunk, 0)
            for k in range(2):
                panel = slots[slot, k * B:(k + 1) * B, :]
                left = slots[slot, 2 * B:2 * B + H, k * H:(k + 1) * H]
                folded = slots[slot, 2 * B + H:3 * B, k * H:(k + 1) * H].astype(F32)
                diagonal = slots[slot, 3 * B:ROWS, k * H:(k + 1) * H].astype(F32)[0:1, :]
                first = jnp.where(tri, folded, 0.0).astype(BF16)
                second = jnp.where(even, diagonal, jnp.where(above, 0.0, folded.T)).astype(BF16)
                v = jnp.concatenate(
                    [jnp.concatenate([first, jnp.zeros((H, H), BF16)], axis=1),
                     jnp.concatenate([left, second], axis=1)], axis=0)
                own_ref[slot, k] = lax.dot_general(
                    v, v, (((0,), (0,)), ((), ())), preferred_element_type=F32)
                carried = jnp.dot(panel, v, preferred_element_type=F32)
                ch, cl = split(carried)
                th, tl = split(carried.T)
                left_ref[slot, k] = jnp.concatenate([th, tl, th], axis=1)
                right_ref[slot, k] = jnp.concatenate([ch, ch, cl], axis=0)
        return carry

    chain_slot = (T0, T1, 2 + z % 2, TOWN, D0, jnp.where(y == 0, RX, Y0), Y1, RX, R1,
                  jnp.where(x == 1, R1, OWN))
    chain_on = (z >= 0, z % 2 == 1, (z // 2) % 2 == 1, z >= 4, c == 1, y >= 0, y == 3, y >= 1,
                x == 3, x >= 1)
    chain_at = (at_slot[T0], at_slot[T1], jnp.where(z % 2 == 0, at_slot[T2], at_slot[T3]), at_slot[TOWN],
                at_slot[D0], jnp.where(y == 0, at_slot[RX], at_slot[Y0]), at_slot[Y1], at_slot[RX],
                at_slot[R1], jnp.where(x == 1, at_slot[R1], at_slot[OWN]))
    ready, latest = [], jnp.int32(0)
    for s in range(10):
        latest = jnp.where(chain_on[s], jnp.maximum(latest, chain_at[s]), latest)
        ready.append(latest)

    def step(s, carry):
        slot = pick(chain_slot, s)

        @pl.when(pick([flag.astype(jnp.int32) for flag in chain_on], s) == 1)
        def _():
            above0, above1 = x_ref[0], x_ref[1]
            for k in range(2):
                tile = slots[slot, 3 * B:ROWS, k * H:(k + 1) * H].astype(F32)
                second = tile[1:2, 0:1] > 0.5
                xh, xl = split(jnp.where(second, above1, above0))
                u = jnp.dot(left_ref[slot, k], jnp.concatenate([xh, xh, xl], axis=0),
                            preferred_element_type=F32)
                uh, ul = split(u)
                x_ref[k] = own_ref[slot, k] + jnp.dot(
                    jnp.concatenate([uh, ul, uh], axis=1), right_ref[slot, k],
                    preferred_element_type=F32)

        @pl.when(s == 3)
        def _():
            top_ref[0] = x_ref[...]
        return carry

    def relay(t, carry):
        prepared, done = carry

        for at, (slot, depth, member, first, end, needed, outs) in enumerate(zflows):
            late_by = t - ZHOP * depth
            j = late_by // ZSTEP

            @pl.when(member & (depth > 0) & (late_by % ZSTEP == 0) & (j >= first) & (j < end))
            def _():
                k = c * ZCH + j
                arrived(slot, k, 2 * ZCH)
                for sid, where, when, lo, hi in outs:
                    @pl.when(when)
                    def _():
                        copy(slot, slot, k, sid, where, 2 * ZCH).start()

                @pl.when(needed)
                def _():
                    copy(slot, slot, k, S_D0 + at, other, 2 * ZCH).start()

        for slot, depth, member, outs in pflows:
            k = t - depth

            @pl.when(member & (depth > 0) & (k >= 0) & (k < CH) & either([o[3] for o in outs]))
            def _():
                arrived(slot, k)
                for dst, sid, where, when in outs:
                    @pl.when(when)
                    def _():
                        copy(slot, dst, k, sid, where).start()

        def so_far(times):
            count = jnp.int32(0)
            for time in times:
                count += (time <= t).astype(jnp.int32)
            return count

        now = so_far(prep_ready)
        lax.fori_loop(prepared, now, prepare, 0)
        count = so_far(ready)
        count = jnp.where(t >= LAST, 10, jnp.minimum(count, done + PACE))
        lax.fori_loop(done, count, step, 0)
        return now, count

    lax.fori_loop(0, LAST + 1, relay, (jnp.int32(0), jnp.int32(0)))
    sub_ref[0, 0] = x_ref[...]

    def gone(sid, rows):
        part = slots.at[0, pl.ds(0, rows), :]
        pltpu.make_async_remote_copy(
            src_ref=part, dst_ref=part, send_sem=send_sem.at[sid], recv_sem=recv_sem.at[0, 0],
            device_id=other, device_id_type=MESH).wait_send()

    for at, (slot, depth, member, first, end, needed, outs) in enumerate(zflows):
        for sid, where, when, lo, hi in outs:
            @pl.when(member & when)
            def _():
                gone(sid, (hi - lo) * (ZROWS // 2 // ZCH))

        @pl.when(needed & (depth > 0))
        def _():
            gone(S_D0 + at, ZROWS // 2)

    streams = {}
    for slot, depth, member, outs in pflows:
        for dst, sid, where, when in outs:
            streams.setdefault(sid, []).append(member & when)
    for sid, flags in streams.items():
        @pl.when(either(flags))
        def _():
            gone(sid, ROWS)


def on_device(root_sigma, top_inv, top_panels, top_parents, sub_inv, sub_panels, sub_parents):
    vmem = pl.BlockSpec(memory_space=pltpu.VMEM)
    hbm = pl.BlockSpec(memory_space=pltpu.HBM)
    arrays = [pltpu.with_memory_space_constraint(a, pltpu.HBM) for a in
              (root_sigma, top_inv, top_panels, top_parents, sub_inv, sub_panels, sub_parents)]
    return pl.pallas_call(
        kernel,
        out_shape=(jax.ShapeDtypeStruct((1, 1, 2, B, B), F32),
                   jax.ShapeDtypeStruct((1, 2, B, B), F32)),
        in_specs=[hbm] * 7,
        out_specs=(vmem, vmem),
        scratch_shapes=[
            pltpu.VMEM((NSLOT, ZROWS, B), BF16),
            pltpu.VMEM((2, B, B), F32),
            pltpu.VMEM((NSLOT, 2, B, B), F32),
            pltpu.VMEM((NSLOT, 2, B, 3 * B), BF16),
            pltpu.VMEM((NSLOT, 2, 3 * B, B), BF16),
            pltpu.VMEM((2, 2, 2, H, H), BF16),
            pltpu.SMEM((1, 2), jnp.int32),
            pltpu.SMEM((1, 1, 2), jnp.int32),
            pltpu.SemaphoreType.DMA((19,)),
            pltpu.SemaphoreType.DMA((NSEND,)),
            pltpu.SemaphoreType.DMA((NSLOT, max(CH, 2 * ZCH))),
        ],
        compiler_params=pltpu.CompilerParams(
            collective_id=0, has_side_effects=True, vmem_limit_bytes=40 << 20),
    )(*arrays)


def solution(mesh):
    in_specs = (
        P(),
        P("leaf", None, None, None),
        P("leaf", None, None, None),
        P("leaf", None),
        P("leaf", "blk", None, None, None),
        P("leaf", "blk", None, None, None),
        P("leaf", "blk", None),
    )
    out_specs = (P("leaf", "blk", None, None, None), P("leaf", None, None, None))
    return jax.shard_map(
        on_device, mesh=mesh, in_specs=in_specs, out_specs=out_specs, check_vma=False
    )
```
